512 devices in a mesh: row: 32 (over x, y, core), col: 16 (over z).
Axes of the slice: x: 4, y: 4, z: 16, core: 2. Of those that a mesh axis runs over, the one named last changes fastest.
Arguments:
- similarity: float32 [8192, 8192], P('row', 'col'), may hold values from 0.1 to 500
- pattern: int32 [32, 32], P('row', 'col'), may hold values from 0 to 1, as said below
Outputs:
- clustered: float32 [8192, 8192], P('row', 'col')
The draws below stay inside these ranges and needn't reach their ends.
Inputs may be any that keep to these rules, and one draw needn't show every extreme that they name: `pattern`: every diagonal tile (g, g) is stored.
All inputs are finite; a program needn't handle non-finite values.
Results may differ from the reference program's by a relative error of at most 0.0003.
Values may be sent and summed in bfloat16 or wider, within the bound.
A program may use at most 64 MiB of HBM per device.

```python
import math
import jax
import jax.numpy as jnp
from jax import lax

TILE = 256
ITERS = 1
NT = 32
NV = 8192


def draw_similarity(key, part):
    first = jax.random.fold_in(key, 11)
    second = jax.random.fold_in(key, 12)
    third = jax.random.fold_in(key, 13)
    place = jnp.arange(NV).astype(jnp.float32) / NV
    base = jax.random.uniform(first, (NV, NV), jnp.float32, 0.5, 1.5)
    row_scale = jnp.exp(math.log(3.0) * place) * jnp.exp(jax.random.uniform(second, (NV,), jnp.float32, 0.0, math.log(10.0)))
    col_scale = jnp.exp(jax.random.uniform(third, (NV,), jnp.float32, 0.0, math.log(10.0)))
    return base * row_scale[:, None] * col_scale[None, :]


def draw_pattern(key, part):
    picks = jax.random.randint(jax.random.fold_in(key, 21), (NT, NT), 0, 8)
    stored = (picks < 3).astype(jnp.int32)
    index = jnp.arange(NT)
    diagonal = (index[:, None] == index[None, :]).astype(jnp.int32)
    return jnp.maximum(stored, diagonal)


def setup_inputs(seed: int = 0) -> dict:
    key_list = jax.random.split(jax.random.key(seed), 3)
    similarity = draw_similarity(jax.random.fold_in(key_list[2], 71), 0)
    pattern = draw_pattern(jax.random.fold_in(key_list[2], 71), 0)
    return {"similarity": similarity, "pattern": pattern}


def spread(pattern):
    rows, cols = pattern.shape
    values = pattern.astype(jnp.float32)
    return jnp.broadcast_to(values[:, None, :, None], (rows, TILE, cols, TILE)).reshape(rows * TILE, cols * TILE)


def reference(similarity, pattern):
    cells = spread(pattern)
    held = similarity * cells
    matrix = held * (NV / jnp.sum(held, axis=0))[None, :]
    for step in range(ITERS):
        operand = lax.optimization_barrier(matrix.astype(jnp.bfloat16)).astype(jnp.float32)
        expanded = jnp.dot(operand, operand, precision=lax.Precision.HIGHEST, preferred_element_type=jnp.float32) * cells
        inflated = expanded * expanded
        matrix = inflated * (NV / jnp.sum(inflated, axis=0))[None, :]
    return matrix
```

```python
import jax
import jax.numpy as jnp
from jax import lax
from jax.experimental import pallas as pl
from jax.experimental.pallas import tpu as pltpu
from jax.sharding import PartitionSpec as P

MESH = pl.DeviceIdType.MESH
TILE = 256
NX, NY, NZ = 4, 4, 16
HALF = TILE // 2

F_OFF = (0, -1, 1, -2)
FORWARD = (1, -1, 1, -1)


def kernel(
    sim_hbm, pat_ref, out_ref,
    sim, left, right, acc, p1, p2, p3, p4,
    in_sem, z_send, z_recv, f_send, f_recv, s_send, s_recv, d_send, d_recv,
    p_send, p_recv,
):
    row = lax.axis_index("row")
    z = lax.axis_index("col")
    core = lax.rem(row, 2)
    chip = row // 2
    y = lax.rem(chip, NY)
    x = chip // NY
    total_rows = float(NX * NY * 2 * TILE)

    load = pltpu.make_async_copy(sim_hbm, sim, in_sem)
    load.start()

    def row_of(xx, yy, cc):
        return (xx * NY + yy) * 2 + cc

    def at(df, ds, cc):
        dx = df * (1 - cc) + ds * cc
        dy = df * cc + ds * (1 - cc)
        return row_of(lax.rem(x + dx + NX, NX), lax.rem(y + dy + NY, NY), cc)

    x_peers = [
        row_of(lax.rem(x + dx, NX), y, lax.rem(core + dc, 2))
        for dx in range(NX) for dc in range(2) if dx or dc
    ]
    y_peers = [row_of(x, lax.rem(y + dy, NY), core) for dy in range(1, NY)]
    z_next = lax.rem(z + 1, NZ)
    z_prev = lax.rem(z + NZ - 1, NZ)
    sibling = row_of(x, y, 1 - core)

    barrier = pltpu.get_barrier_semaphore()
    for peer in x_peers + y_peers:
        pl.semaphore_signal(barrier, inc=1, device_id=(peer, z), device_id_type=MESH)
    for peer in (z_next, z_prev):
        pl.semaphore_signal(barrier, inc=1, device_id=(row, peer), device_id_type=MESH)
    p_left = pat_ref[0, 0].astype(jnp.float32)
    p_right = pat_ref[0, 1].astype(jnp.float32)
    load.wait()
    sim[:, :TILE] = sim[:, :TILE] * p_left
    sim[:, TILE:] = sim[:, TILE:] * p_right
    part = jnp.sum(sim[...], axis=0, keepdims=True)
    pl.semaphore_wait(barrier, len(x_peers) + len(y_peers) + 2)

    pending = []

    def send(src, dst, send_sem, recv_sem, to):
        copy = pltpu.make_async_remote_copy(
            src_ref=src, dst_ref=dst, send_sem=send_sem, recv_sem=recv_sem,
            device_id=to, device_id_type=MESH,
        )
        copy.start()
        pending.append(copy)
        return copy

    def plane_sum(value, first, second, base):
        slot = x * 2 + core
        first[slot] = value
        copies = [
            send(first.at[slot], first.at[slot], p_send.at[base + i], p_recv.at[base + i], (peer, z))
            for i, peer in enumerate(x_peers)
        ]
        for copy in copies:
            copy.wait_recv()
        second[y] = jnp.sum(first[...], axis=0)
        copies = [
            send(second.at[y], second.at[y], p_send.at[base + 7 + i], p_recv.at[base + 7 + i], (peer, z))
            for i, peer in enumerate(y_peers)
        ]
        for copy in copies:
            copy.wait_recv()
        return jnp.sum(second[...], axis=0)

    total = plane_sum(part, p1, p2, 0)
    operand = (sim[...] * (total_rows / total)).astype(jnp.bfloat16)
    left[z] = operand

    def block(r):
        return right.at[r // 2, pl.ds(lax.rem(r, 2) * TILE, TILE)]

    right[chip, pl.ds(core * TILE, TILE)] = operand

    z_copies = {}

    def z_hop(way, j):
        origin = lax.rem(z - way * (j // 2) + NZ, NZ)
        half = j % 2 if way > 0 else 1 - j % 2
        ref = left.at[origin, pl.ds(half * HALF, HALF)]
        w = 0 if way > 0 else 1
        z_copies[way, j] = send(ref, ref, z_send.at[w, j], z_recv.at[w, j], (row, z_next if way > 0 else z_prev))

    plane = {}

    def plane_hop(df, ds, sems, to_f, to_s, key):
        ref = block(at(df, ds, core))
        plane[key] = send(ref, ref, sems[0], sems[1], (at(to_f, to_s, core), z))

    def f_hop(i, df, way):
        plane_hop(df, 0, (f_send.at[i], f_recv.at[i]), way, 0, ("f", i))

    def s_hop(g, i, ds, way):
        plane_hop(F_OFF[g], ds, (s_send.at[g, i], s_recv.at[g, i]), 0, way, ("s", g, i))

    to_sibling = []

    def share(df, ds):
        i = len(to_sibling)
        ref = block(at(df, ds, core))
        to_sibling.append(send(ref, ref, d_send.at[i], d_recv.at[i], (sibling, z)))

    def spread(g):
        s_hop(g, 0, 0, 1)
        s_hop(g, 1, 0, -1)

    def arrive(key):
        plane[key].wait_recv()
        if key[0] == "f":
            i = key[1]
            if i == 0:
                f_hop(2, -1, 1)
                share(-1, 0)
                spread(1)
            elif i == 1:
                share(1, 0)
                spread(2)
            else:
                share(-2, 0)
                spread(3)
        else:
            _, g, i = key
            way = FORWARD[g]
            if i == 2:
                share(F_OFF[g], -2 * way)
                return
            ds = -1 if i == 0 else 1
            if ds == -way:
                s_hop(g, 2, ds, way)
            share(F_OFF[g], ds)

    z_hop(1, 0)
    z_hop(-1, 0)
    f_hop(0, 0, 1)
    f_hop(1, 0, -1)
    spread(0)
    z_hop(1, 1)
    z_hop(-1, 1)
    share(0, 0)

    def products(first, count):
        def body(i, carry):
            k = lax.rem(z + first + NZ + i, NZ)
            acc[...] += jnp.dot(left[k], right[k], preferred_element_type=jnp.float32)
            return carry
        lax.fori_loop(0, count, body, 0)

    acc[...] = jnp.zeros_like(acc)

    after = {
        1: [("f", 0), ("f", 1), ("s", 0, 0), ("s", 0, 1)],
        3: [("s", 1, 1)],
        4: [("f", 2), ("s", 0, 2), ("s", 2, 1)],
        5: [("s", 1, 0), ("s", 1, 2)],
        6: [("s", 3, 1), ("s", 2, 0)],
        7: [("s", 3, 0), ("s", 3, 2)],
        8: [("s", 2, 2)],
    }
    compute = {
        10: [(-1, 3)],
        11: [(2, 2), (-3, 2)],
        12: [(4, 2), (-5, 2)],
        13: [(6, 2), (-7, 2)],
        14: [(8, 1)],
    }
    last = NZ - 2
    for j in range(last + 1):
        for way in (1, -1):
            z_copies[way, j].wait_recv()
            if j + 2 <= last:
                z_hop(way, j + 2)
        for key in after.get(j, ()):
            arrive(key)
        if j == 9:
            for copy in to_sibling:
                copy.wait_recv()
        for first, count in compute.get(j, ()):
            products(first, count)

    left_part = acc[:, :TILE] * p_left
    right_part = acc[:, TILE:] * p_right
    acc[:, :TILE] = left_part * left_part
    acc[:, TILE:] = right_part * right_part
    sums = plane_sum(jnp.sum(acc[...], axis=0, keepdims=True), p3, p4, 10)
    out_ref[...] = acc[...] * (total_rows / sums)

    for copy in pending:
        copy.wait_send()


def shards(similarity, pattern):
    rows, columns = similarity.shape
    dma = pltpu.SemaphoreType.DMA
    return pl.pallas_call(
        kernel,
        out_shape=jax.ShapeDtypeStruct((rows, columns), jnp.float32),
        in_specs=[
            pl.BlockSpec(memory_space=pl.ANY),
            pl.BlockSpec(memory_space=pltpu.SMEM),
        ],
        out_specs=pl.BlockSpec(memory_space=pltpu.VMEM),
        scratch_shapes=[
            pltpu.VMEM((rows, columns), jnp.float32),
            pltpu.VMEM((NZ, rows, columns), jnp.bfloat16),
            pltpu.VMEM((NX * NY, 2 * rows, columns), jnp.bfloat16),
            pltpu.VMEM((rows, columns), jnp.float32),
            pltpu.VMEM((8, 1, columns), jnp.float32),
            pltpu.VMEM((4, 1, columns), jnp.float32),
            pltpu.VMEM((8, 1, columns), jnp.float32),
            pltpu.VMEM((4, 1, columns), jnp.float32),
            dma, dma((2, NZ - 1)), dma((2, NZ - 1)), dma((3,)), dma((3,)),
            dma((4, 3)), dma((4, 3)), dma((NX * NY,)), dma((NX * NY,)),
            dma((20,)), dma((20,)),
        ],
        compiler_params=pltpu.CompilerParams(collective_id=0, has_side_effects=True),
    )(similarity, pattern)


def solution(mesh):
    placed = (P("row", "col"), P("row", "col"))
    return jax.shard_map(
        shards, mesh=mesh, in_specs=placed, out_specs=P("row", "col"), check_vma=False
    )
```

```python
import jax
import jax.numpy as jnp
from jax import lax
from jax.experimental import pallas as pl
from jax.experimental.pallas import tpu as pltpu
from jax.sharding import PartitionSpec as P

MESH = pl.DeviceIdType.MESH
TILE = 256
NX, NY, NZ = 4, 4, 16
HALF = TILE // 2

F_OFF = (0, -1, 1, -2)
FORWARD = (1, -1, 1, -1)


def kernel(
    sim_hbm, pat_ref, acc, scale_ref,
    sim, left, right, p1, p2,
    in_sem, z_send, z_recv, f_send, f_recv, s_send, s_recv, d_send, d_recv,
    p_send, p_recv,
):
    row = lax.axis_index("row")
    z = lax.axis_index("col")
    core = lax.rem(row, 2)
    chip = row // 2
    y = lax.rem(chip, NY)
    x = chip // NY
    total_rows = float(NX * NY * 2 * TILE)

    load = pltpu.make_async_copy(sim_hbm, sim, in_sem)
    load.start()

    def row_of(xx, yy, cc):
        return (xx * NY + yy) * 2 + cc

    def at(df, ds, cc):
        dx = df * (1 - cc) + ds * cc
        dy = df * cc + ds * (1 - cc)
        return row_of(lax.rem(x + dx + NX, NX), lax.rem(y + dy + NY, NY), cc)

    peers = [
        row_of(lax.rem(x + dx, NX), lax.rem(y + dy, NY), lax.rem(core + dc, 2))
        for dx in (2, 1, 3, 0) for dy in (2, 1, 3, 0) for dc in (0, 1) if dx or dy or dc
    ]
    z_next = lax.rem(z + 1, NZ)
    z_prev = lax.rem(z + NZ - 1, NZ)
    sibling = row_of(x, y, 1 - core)

    barrier = pltpu.get_barrier_semaphore()
    for peer in peers:
        pl.semaphore_signal(barrier, inc=1, device_id=(peer, z), device_id_type=MESH)
    for peer in (z_next, z_prev):
        pl.semaphore_signal(barrier, inc=1, device_id=(row, peer), device_id_type=MESH)
    p_left = pat_ref[0, 0].astype(jnp.float32)
    p_right = pat_ref[0, 1].astype(jnp.float32)
    load.wait()
    sim[:, :TILE] = sim[:, :TILE] * p_left
    sim[:, TILE:] = sim[:, TILE:] * p_right
    part = jnp.sum(sim[...], axis=0, keepdims=True)
    pl.semaphore_wait(barrier, len(peers) + 2)

    pending = []

    def send(src, dst, send_sem, recv_sem, to):
        copy = pltpu.make_async_remote_copy(
            src_ref=src, dst_ref=dst, send_sem=send_sem, recv_sem=recv_sem,
            device_id=to, device_id_type=MESH,
        )
        copy.start()
        pending.append(copy)
        return copy

    def plane_sum(value, parts, base):
        parts[row] = value
        copies = [
            send(parts.at[row], parts.at[row], p_send.at[base + i], p_recv.at[base + i], (peer, z))
            for i, peer in enumerate(peers)
        ]
        for copy in copies:
            copy.wait_recv()
        return jnp.sum(parts[...], axis=0)

    total = plane_sum(part, p1, 0)
    operand = (sim[...] * (total_rows / total)).astype(jnp.bfloat16)
    left[z] = operand

    def block(r):
        return right.at[r // 2, pl.ds(lax.rem(r, 2) * TILE, TILE)]

    right[chip, pl.ds(core * TILE, TILE)] = operand

    z_copies = {}

    def z_hop(way, j):
        origin = lax.rem(z - way * (j // 2) + NZ, NZ)
        half = j % 2 if way > 0 else 1 - j % 2
        ref = left.at[origin, pl.ds(half * HALF, HALF)]
        w = 0 if way > 0 else 1
        z_copies[way, j] = send(ref, ref, z_send.at[w, j], z_recv.at[w, j], (row, z_next if way > 0 else z_prev))

    plane = {}

    def plane_hop(df, ds, sems, to_f, to_s, key):
        ref = block(at(df, ds, core))
        plane[key] = send(ref, ref, sems[0], sems[1], (at(to_f, to_s, core), z))

    def f_hop(i, df, way):
        plane_hop(df, 0, (f_send.at[i], f_recv.at[i]), way, 0, ("f", i))

    def s_hop(g, i, ds, way):
        plane_hop(F_OFF[g], ds, (s_send.at[g, i], s_recv.at[g, i]), 0, way, ("s", g, i))

    to_sibling = []

    def share(df, ds):
        i = len(to_sibling)
        ref = block(at(df, ds, core))
        to_sibling.append(send(ref, ref, d_send.at[i], d_recv.at[i], (sibling, z)))

    def spread(g):
        s_hop(g, 0, 0, 1)
        s_hop(g, 1, 0, -1)

    def arrive(key):
        plane[key].wait_recv()
        if key[0] == "f":
            i = key[1]
            if i == 0:
                f_hop(2, -1, 1)
                share(-1, 0)
                spread(1)
            elif i == 1:
                share(1, 0)
                spread(2)
            else:
                share(-2, 0)
                spread(3)
        else:
            _, g, i = key
            way = FORWARD[g]
            if i == 2:
                share(F_OFF[g], -2 * way)
                return
            ds = -1 if i == 0 else 1
            if ds == -way:
                s_hop(g, 2, ds, way)
            share(F_OFF[g], ds)

    z_hop(1, 0)
    z_hop(-1, 0)
    f_hop(0, 0, 1)
    f_hop(1, 0, -1)
    spread(0)
    z_hop(1, 1)
    z_hop(-1, 1)
    share(0, 0)

    def products(first, count):
        def body(i, carry):
            k = lax.rem(z + first + NZ + i, NZ)
            acc[...] += jnp.dot(left[k], right[k], preferred_element_type=jnp.float32)
            return carry
        lax.fori_loop(0, count, body, 0)

    acc[...] = jnp.zeros_like(acc)

    after = {
        1: [("f", 0), ("f", 1), ("s", 0, 0), ("s", 0, 1)],
        3: [("s", 1, 1)],
        4: [("f", 2), ("s", 0, 2), ("s", 2, 1)],
        5: [("s", 1, 0), ("s", 1, 2)],
        6: [("s", 3, 1), ("s", 2, 0)],
        7: [("s", 3, 0), ("s", 3, 2)],
        8: [("s", 2, 2)],
    }
    compute = {
        10: [(-1, 3)],
        11: [(2, 2), (-3, 2)],
        12: [(4, 2), (-5, 2)],
        13: [(6, 2), (-7, 2)],
        14: [(8, 1)],
    }
    last = NZ - 2
    for j in range(last + 1):
        for way in (1, -1):
            z_copies[way, j].wait_recv()
            if j + 2 <= last:
                z_hop(way, j + 2)
        for key in after.get(j, ()):
            arrive(key)
        if j == 9:
            for copy in to_sibling:
                copy.wait_recv()
        for first, count in compute.get(j, ()):
            products(first, count)

    left_part = acc[:, :TILE] * p_left
    right_part = acc[:, TILE:] * p_right
    acc[:, :TILE] = left_part * left_part
    acc[:, TILE:] = right_part * right_part
    sums = plane_sum(jnp.sum(acc[...], axis=0, keepdims=True), p2, len(peers))
    scale_ref[...] = total_rows / sums

    for copy in pending:
        copy.wait_send()


def shards(similarity, pattern):
    rows, columns = similarity.shape
    dma = pltpu.SemaphoreType.DMA
    planes = NX * NY * 2
    inflated, scale = pl.pallas_call(
        kernel,
        out_shape=(
            pltpu.VMEM((rows, columns), jnp.float32),
            pltpu.VMEM((1, columns), jnp.float32),
        ),
        in_specs=[
            pl.BlockSpec(memory_space=pl.ANY),
            pl.BlockSpec(memory_space=pltpu.SMEM),
        ],
        out_specs=(pl.BlockSpec(memory_space=pltpu.VMEM),) * 2,
        scratch_shapes=[
            pltpu.VMEM((rows, columns), jnp.float32),
            pltpu.VMEM((NZ, rows, columns), jnp.bfloat16),
            pltpu.VMEM((NX * NY, 2 * rows, columns), jnp.bfloat16),
            pltpu.VMEM((planes, 1, columns), jnp.float32),
            pltpu.VMEM((planes, 1, columns), jnp.float32),
            dma, dma((2, NZ - 1)), dma((2, NZ - 1)), dma((3,)), dma((3,)),
            dma((4, 3)), dma((4, 3)), dma((NX * NY,)), dma((NX * NY,)),
            dma((2 * planes - 2,)), dma((2 * planes - 2,)),
        ],
        compiler_params=pltpu.CompilerParams(collective_id=0, has_side_effects=True),
    )(similarity, pattern)
    return inflated * scale


def solution(mesh):
    placed = (P("row", "col"), P("row", "col"))
    return jax.shard_map(
        shards, mesh=mesh, in_specs=placed, out_specs=P("row", "col"), check_vma=False
    )
```

```python
import jax
import jax.numpy as jnp
from jax import lax
from jax.experimental import pallas as pl
from jax.experimental.pallas import tpu as pltpu
from jax.sharding import PartitionSpec as P

MESH = pl.DeviceIdType.MESH
TILE = 256
NX, NY, NZ = 4, 4, 16
HALF = TILE // 2

F_OFF = (0, -1, 1, -2)
FORWARD = (1, -1, 1, -1)


def kernel(
    sim_hbm, pat_ref, acc, scale_ref,
    sim, left, right, p1, p2, raw, scales,
    in_sem, z_send, z_recv, r_send, r_recv, c_send, c_recv, f_send, f_recv, s_send, s_recv, d_send, d_recv,
    p_send, p_recv,
):
    row = lax.axis_index("row")
    z = lax.axis_index("col")
    core = lax.rem(row, 2)
    chip = row // 2
    y = lax.rem(chip, NY)
    x = chip // NY
    total_rows = float(NX * NY * 2 * TILE)

    load = pltpu.make_async_copy(sim_hbm, sim, in_sem)
    load.start()

    def row_of(xx, yy, cc):
        return (xx * NY + yy) * 2 + cc

    def at(df, ds, cc):
        dx = df * (1 - cc) + ds * cc
        dy = df * cc + ds * (1 - cc)
        return row_of(lax.rem(x + dx + NX, NX), lax.rem(y + dy + NY, NY), cc)

    peers = [
        row_of(lax.rem(x + dx, NX), lax.rem(y + dy, NY), lax.rem(core + dc, 2))
        for dx in (2, 1, 3, 0) for dy in (2, 1, 3, 0) for dc in (0, 1) if dx or dy or dc
    ]
    z_next = lax.rem(z + 1, NZ)
    z_prev = lax.rem(z + NZ - 1, NZ)
    sibling = row_of(x, y, 1 - core)

    barrier = pltpu.get_barrier_semaphore()
    for peer in peers:
        pl.semaphore_signal(barrier, inc=1, device_id=(peer, z), device_id_type=MESH)
    for peer in (z_next, z_prev):
        pl.semaphore_signal(barrier, inc=1, device_id=(row, peer), device_id_type=MESH)
    cells = jnp.where(
        lax.broadcasted_iota(jnp.int32, (1, sim.shape[1]), 1) < TILE, pat_ref[0, 0], pat_ref[0, 1]
    ).astype(jnp.float32)
    load.wait()
    part = jnp.sum(sim[...], axis=0, keepdims=True) * cells
    pl.semaphore_wait(barrier, len(peers) + 2)

    pending = []

    def send(src, dst, send_sem, recv_sem, to):
        copy = pltpu.make_async_remote_copy(
            src_ref=src, dst_ref=dst, send_sem=send_sem, recv_sem=recv_sem,
            device_id=to, device_id_type=MESH,
        )
        copy.start()
        pending.append(copy)
        return copy

    def plane_sum(value, parts, base):
        parts[row] = value
        copies = [
            send(parts.at[row], parts.at[row], p_send.at[base + i], p_recv.at[base + i], (peer, z))
            for i, peer in enumerate(peers)
        ]
        for copy in copies:
            copy.wait_recv()
        return jnp.sum(parts[...], axis=0)

    ways = ((1, z_next), (-1, z_prev))
    raw_copies = [
        send(sim.at[pl.ds(w * HALF, HALF)], raw.at[w], r_send.at[w], r_recv.at[w], (row, peer))
        for w, (_, peer) in enumerate(ways)
    ]

    total = plane_sum(part, p1, 0)
    scale = cells * (total_rows / total)
    scales[2] = scale
    scale_copies = [
        send(scales.at[2], scales.at[w], c_send.at[w], c_recv.at[w], (row, peer))
        for w, (_, peer) in enumerate(ways)
    ]
    operand = (sim[...] * scale).astype(jnp.bfloat16)
    left[z] = operand

    def block(r):
        return right.at[r // 2, pl.ds(lax.rem(r, 2) * TILE, TILE)]

    right[chip, pl.ds(core * TILE, TILE)] = operand

    last = NZ - 2
    z_copies = {}

    def z_hop(way, j):
        origin = lax.rem(z - way * (j // 2) + NZ, NZ)
        half = j % 2 if way > 0 else 1 - j % 2
        ref = left.at[origin, pl.ds(half * HALF, HALF)]
        w = 0 if way > 0 else 1
        z_copies[way, j] = send(ref, ref, z_send.at[w, j], z_recv.at[w, j], (row, z_next if way > 0 else z_prev))

    def z_take(way, j):
        if j == 0:
            w = 0 if way > 0 else 1
            raw_copies[w].wait_recv()
            scale_copies[w].wait_recv()
            left[z_prev if way > 0 else z_next, pl.ds(w * HALF, HALF)] = (raw[w] * scales[w]).astype(jnp.bfloat16)
        else:
            z_copies[way, j].wait_recv()
        if j + 2 <= last:
            z_hop(way, j + 2)

    plane = {}

    def plane_hop(df, ds, sems, to_f, to_s, key):
        ref = block(at(df, ds, core))
        plane[key] = send(ref, ref, sems[0], sems[1], (at(to_f, to_s, core), z))

    def f_hop(i, df, way):
        plane_hop(df, 0, (f_send.at[i], f_recv.at[i]), way, 0, ("f", i))

    def s_hop(g, i, ds, way):
        plane_hop(F_OFF[g], ds, (s_send.at[g, i], s_recv.at[g, i]), 0, way, ("s", g, i))

    to_sibling = []

    def share(df, ds):
        i = len(to_sibling)
        ref = block(at(df, ds, core))
        to_sibling.append(send(ref, ref, d_send.at[i], d_recv.at[i], (sibling, z)))

    def spread(g):
        s_hop(g, 0, 0, 1)
        s_hop(g, 1, 0, -1)

    def arrive(key):
        plane[key].wait_recv()
        if key[0] == "f":
            i = key[1]
            if i == 0:
                f_hop(2, -1, 1)
                share(-1, 0)
                spread(1)
            elif i == 1:
                share(1, 0)
                spread(2)
            else:
                share(-2, 0)
                spread(3)
        else:
            _, g, i = key
            way = FORWARD[g]
            if i == 2:
                share(F_OFF[g], -2 * way)
                return
            ds = -1 if i == 0 else 1
            if ds == -way:
                s_hop(g, 2, ds, way)
            share(F_OFF[g], ds)

    z_hop(1, 1)
    z_hop(-1, 1)
    f_hop(0, 0, 1)
    f_hop(1, 0, -1)
    spread(0)
    share(0, 0)

    def products(first, count):
        def body(i, carry):
            k = lax.rem(z + first + NZ + i, NZ)
            acc[...] += jnp.dot(left[k], right[k], preferred_element_type=jnp.float32)
            return carry
        lax.fori_loop(0, count, body, 0)

    acc[...] = jnp.zeros_like(acc)

    after = {
        3: [("f", 0), ("f", 1), ("s", 0, 0), ("s", 0, 1)],
        5: [("s", 1, 1)],
        6: [("f", 2), ("s", 0, 2), ("s", 2, 1)],
        7: [("s", 1, 0), ("s", 1, 2)],
        8: [("s", 3, 1), ("s", 2, 0)],
        9: [("s", 3, 0), ("s", 3, 2)],
        10: [("s", 2, 2)],
    }
    compute = {
        11: [(-2, 5)],
        12: [(3, 3), (-5, 3)],
        13: [(6, 2), (-7, 2)],
        14: [(8, 1)],
    }
    for j in range(last + 1):
        z_take(1, j)
        z_take(-1, j)
        for key in after.get(j, ()):
            arrive(key)
        if j == 11:
            for copy in to_sibling:
                copy.wait_recv()
        for first, count in compute.get(j, ()):
            products(first, count)

    acc[...] = jnp.square(acc[...] * cells)
    sums = plane_sum(jnp.sum(acc[...], axis=0, keepdims=True), p2, len(peers))
    scale_ref[...] = total_rows / sums

    for copy in pending:
        copy.wait_send()


def shards(similarity, pattern):
    rows, columns = similarity.shape
    dma = pltpu.SemaphoreType.DMA
    planes = NX * NY * 2
    inflated, scale = pl.pallas_call(
        kernel,
        out_shape=(
            pltpu.VMEM((rows, columns), jnp.float32),
            pltpu.VMEM((1, columns), jnp.float32),
        ),
        in_specs=[
            pl.BlockSpec(memory_space=pl.ANY),
            pl.BlockSpec(memory_space=pltpu.SMEM),
        ],
        out_specs=(pl.BlockSpec(memory_space=pltpu.VMEM),) * 2,
        scratch_shapes=[
            pltpu.VMEM((rows, columns), jnp.float32),
            pltpu.VMEM((NZ, rows, columns), jnp.bfloat16),
            pltpu.VMEM((NX * NY, 2 * rows, columns), jnp.bfloat16),
            pltpu.VMEM((planes, 1, columns), jnp.float32),
            pltpu.VMEM((planes, 1, columns), jnp.float32),
            pltpu.VMEM((2, HALF, columns), jnp.float32),
            pltpu.VMEM((3, 1, columns), jnp.float32),
            dma, dma((2, NZ - 1)), dma((2, NZ - 1)), dma((2,)), dma((2,)), dma((2,)), dma((2,)),
            dma((3,)), dma((3,)),
            dma((4, 3)), dma((4, 3)), dma((NX * NY,)), dma((NX * NY,)),
            dma((2 * planes - 2,)), dma((2 * planes - 2,)),
        ],
        compiler_params=pltpu.CompilerParams(collective_id=0, has_side_effects=True),
    )(similarity, pattern)
    return inflated * scale


def solution(mesh):
    placed = (P("row", "col"), P("row", "col"))
    return jax.shard_map(
        shards, mesh=mesh, in_specs=placed, out_specs=P("row", "col"), check_vma=False
    )
```

```python
import jax
import jax.numpy as jnp
from jax import lax
from jax.experimental import pallas as pl
from jax.experimental.pallas import tpu as pltpu
from jax.sharding import PartitionSpec as P

MESH = pl.DeviceIdType.MESH
TILE = 256
NX, NY, NZ = 4, 4, 16
HALF = TILE // 2

F_OFF = (0, -1, 1, -2)
FORWARD = (1, -1, 1, -1)


def kernel(
    sim_hbm, pat_ref, acc, scale_ref,
    sim, left, right, p1, p2, raw, scales,
    in_sem, z_send, z_recv, r_send, r_recv, c_send, c_recv, f_send, f_recv, s_send, s_recv, d_send, d_recv,
    p_send, p_recv,
):
    row = lax.axis_index("row")
    z = lax.axis_index("col")
    core = lax.rem(row, 2)
    chip = row // 2
    y = lax.rem(chip, NY)
    x = chip // NY
    total_rows = float(NX * NY * 2 * TILE)

    load = pltpu.make_async_copy(sim_hbm, sim, in_sem)
    load.start()

    def row_of(xx, yy, cc):
        return (xx * NY + yy) * 2 + cc

    def at(df, ds, cc):
        dx = df * (1 - cc) + ds * cc
        dy = df * cc + ds * (1 - cc)
        return row_of(lax.rem(x + dx + NX, NX), lax.rem(y + dy + NY, NY), cc)

    peers = [
        row_of(lax.rem(x + dx, NX), lax.rem(y + dy, NY), lax.rem(core + dc, 2))
        for dx in (2, 1, 3, 0) for dy in (2, 1, 3, 0) for dc in (0, 1) if dx or dy or dc
    ]
    z_next = lax.rem(z + 1, NZ)
    z_prev = lax.rem(z + NZ - 1, NZ)
    sibling = row_of(x, y, 1 - core)

    barrier = pltpu.get_barrier_semaphore()
    for peer in peers:
        pl.semaphore_signal(barrier, inc=1, device_id=(peer, z), device_id_type=MESH)
    for peer in (z_next, z_prev):
        pl.semaphore_signal(barrier, inc=1, device_id=(row, peer), device_id_type=MESH)
    cells = jnp.where(
        lax.broadcasted_iota(jnp.int32, (1, sim.shape[1]), 1) < TILE, pat_ref[0, 0], pat_ref[0, 1]
    ).astype(jnp.float32)
    load.wait()
    part = jnp.sum(sim[...], axis=0, keepdims=True) * cells
    pl.semaphore_wait(barrier, len(peers) + 2)

    pending = []

    def send(src, dst, send_sem, recv_sem, to):
        copy = pltpu.make_async_remote_copy(
            src_ref=src, dst_ref=dst, send_sem=send_sem, recv_sem=recv_sem,
            device_id=to, device_id_type=MESH,
        )
        copy.start()
        pending.append(copy)
        return copy

    def plane_sum(value, parts, base):
        parts[row] = value
        copies = [
            send(parts.at[row], parts.at[row], p_send.at[base + i], p_recv.at[base + i], (peer, z))
            for i, peer in enumerate(peers)
        ]
        if base:
            for copy in pending[:-len(copies)]:
                copy.wait_send()
            del pending[:-len(copies)]
        for copy in copies:
            copy.wait_recv()
        return jnp.sum(parts[...], axis=0)

    ways = ((1, z_next), (-1, z_prev))
    raw_copies = [
        send(sim.at[pl.ds(w * HALF, HALF)], raw.at[w], r_send.at[w], r_recv.at[w], (row, peer))
        for w, (_, peer) in enumerate(ways)
    ]

    total = plane_sum(part, p1, 0)
    scale = cells * (total_rows / total)
    scales[2] = scale
    scale_copies = [
        send(scales.at[2], scales.at[w], c_send.at[w], c_recv.at[w], (row, peer))
        for w, (_, peer) in enumerate(ways)
    ]
    operand = (sim[...] * scale).astype(jnp.bfloat16)
    left[z] = operand

    def block(r):
        return right.at[r // 2, pl.ds(lax.rem(r, 2) * TILE, TILE)]

    right[chip, pl.ds(core * TILE, TILE)] = operand

    last = NZ - 2
    z_copies = {}

    def z_hop(way, j):
        origin = lax.rem(z - way * (j // 2) + NZ, NZ)
        half = j % 2 if way > 0 else 1 - j % 2
        ref = left.at[origin, pl.ds(half * HALF, HALF)]
        w = 0 if way > 0 else 1
        z_copies[way, j] = send(ref, ref, z_send.at[w, j], z_recv.at[w, j], (row, z_next if way > 0 else z_prev))

    def z_take(way, j):
        if j == 0:
            w = 0 if way > 0 else 1
            raw_copies[w].wait_recv()
            scale_copies[w].wait_recv()
            left[z_prev if way > 0 else z_next, pl.ds(w * HALF, HALF)] = (raw[w] * scales[w]).astype(jnp.bfloat16)
        else:
            z_copies[way, j].wait_recv()
        if j + 2 <= last:
            z_hop(way, j + 2)

    plane = {}

    def plane_hop(df, ds, sems, to_f, to_s, key):
        ref = block(at(df, ds, core))
        plane[key] = send(ref, ref, sems[0], sems[1], (at(to_f, to_s, core), z))

    def f_hop(i, df, way):
        plane_hop(df, 0, (f_send.at[i], f_recv.at[i]), way, 0, ("f", i))

    def s_hop(g, i, ds, way):
        plane_hop(F_OFF[g], ds, (s_send.at[g, i], s_recv.at[g, i]), 0, way, ("s", g, i))

    to_sibling = []

    def share(df, ds):
        i = len(to_sibling)
        ref = block(at(df, ds, core))
        to_sibling.append(send(ref, ref, d_send.at[i], d_recv.at[i], (sibling, z)))

    def spread(g):
        s_hop(g, 0, 0, 1)
        s_hop(g, 1, 0, -1)

    def arrive(key):
        plane[key].wait_recv()
        if key[0] == "f":
            i = key[1]
            if i == 0:
                f_hop(2, -1, 1)
                share(-1, 0)
                spread(1)
            elif i == 1:
                share(1, 0)
                spread(2)
            else:
                share(-2, 0)
                spread(3)
        else:
            _, g, i = key
            way = FORWARD[g]
            if i == 2:
                share(F_OFF[g], -2 * way)
                return
            ds = -1 if i == 0 else 1
            if ds == -way:
                s_hop(g, 2, ds, way)
            share(F_OFF[g], ds)

    z_hop(1, 1)
    z_hop(-1, 1)
    f_hop(0, 0, 1)
    f_hop(1, 0, -1)
    spread(0)
    share(0, 0)

    def products(first, count):
        def body(i, carry):
            k = lax.rem(z + first + NZ + i, NZ)
            acc[...] += jnp.dot(left[k], right[k], preferred_element_type=jnp.float32)
            return carry
        lax.fori_loop(0, count, body, 0)

    acc[...] = jnp.zeros_like(acc)

    after = {
        3: [("f", 0), ("f", 1), ("s", 0, 0), ("s", 0, 1)],
        5: [("s", 1, 1)],
        6: [("f", 2), ("s", 0, 2), ("s", 2, 1)],
        7: [("s", 1, 0), ("s", 1, 2)],
        8: [("s", 3, 1), ("s", 2, 0)],
        9: [("s", 3, 0), ("s", 3, 2)],
        10: [("s", 2, 2)],
    }
    compute = {
        11: [(-2, 5)],
        12: [(3, 3), (-5, 3)],
        13: [(6, 2), (-7, 2)],
    }
    for j in range(last + 1):
        z_take(1, j)
        for key in after.get(j, ())[:len(after.get(j, ())) // 2]:
            arrive(key)
        z_take(-1, j)
        for key in after.get(j, ())[len(after.get(j, ())) // 2:]:
            arrive(key)
        if j == 11:
            for copy in to_sibling:
                copy.wait_recv()
        for first, count in compute.get(j, ()):
            products(first, count)

    k = lax.rem(z + NZ // 2, NZ)
    column_sum = jnp.zeros((1, sim.shape[1]), jnp.float32)
    for h in range(2):
        rows = pl.ds(h * HALF, HALF)
        final = acc[rows] + jnp.dot(left[k, rows], right[k], preferred_element_type=jnp.float32)
        final = jnp.square(final * cells)
        acc[rows] = final
        column_sum += jnp.sum(final, axis=0, keepdims=True)
    sums = plane_sum(column_sum, p2, len(peers))
    scale_ref[...] = total_rows / sums

    for copy in pending:
        copy.wait_send()


def shards(similarity, pattern):
    rows, columns = similarity.shape
    dma = pltpu.SemaphoreType.DMA
    planes = NX * NY * 2
    inflated, scale = pl.pallas_call(
        kernel,
        out_shape=(
            pltpu.VMEM((rows, columns), jnp.float32),
            pltpu.VMEM((1, columns), jnp.float32),
        ),
        in_specs=[
            pl.BlockSpec(memory_space=pl.ANY),
            pl.BlockSpec(memory_space=pltpu.SMEM),
        ],
        out_specs=(pl.BlockSpec(memory_space=pltpu.VMEM),) * 2,
        scratch_shapes=[
            pltpu.VMEM((rows, columns), jnp.float32),
            pltpu.VMEM((NZ, rows, columns), jnp.bfloat16),
            pltpu.VMEM((NX * NY, 2 * rows, columns), jnp.bfloat16),
            pltpu.VMEM((planes, 1, columns), jnp.float32),
            pltpu.VMEM((planes, 1, columns), jnp.float32),
            pltpu.VMEM((2, HALF, columns), jnp.float32),
            pltpu.VMEM((3, 1, columns), jnp.float32),
            dma, dma((2, NZ - 1)), dma((2, NZ - 1)), dma((2,)), dma((2,)), dma((2,)), dma((2,)),
            dma((3,)), dma((3,)),
            dma((4, 3)), dma((4, 3)), dma((NX * NY,)), dma((NX * NY,)),
            dma((2 * planes - 2,)), dma((2 * planes - 2,)),
        ],
        compiler_params=pltpu.CompilerParams(collective_id=0, has_side_effects=True),
    )(similarity, pattern)
    return inflated * scale


def solution(mesh):
    placed = (P("row", "col"), P("row", "col"))
    return jax.shard_map(
        shards, mesh=mesh, in_specs=placed, out_specs=P("row", "col"), check_vma=False
    )
```

```python
import jax
import jax.numpy as jnp
from jax import lax
from jax.experimental import pallas as pl
from jax.experimental.pallas import tpu as pltpu
from jax.sharding import PartitionSpec as P

MESH = pl.DeviceIdType.MESH
TILE = 256
NX, NY, NZ = 4, 4, 16
HALF = TILE // 2

F_OFF = (0, -1, 1, -2)
FORWARD = (1, -1, 1, -1)


def kernel(
    sim_hbm, pat_ref, acc, scale_ref,
    sim, left, right, p1, p2, raw, scales,
    in_sem, z_send, z_recv, r_send, r_recv, c_send, c_recv, f_send, f_recv, s_send, s_recv, d_send, d_recv,
    p_send, p_recv,
):
    row = lax.axis_index("row")
    z = lax.axis_index("col")
    core = lax.rem(row, 2)
    chip = row // 2
    y = lax.rem(chip, NY)
    x = chip // NY
    total_rows = float(NX * NY * 2 * TILE)

    load = pltpu.make_async_copy(sim_hbm, sim, in_sem)
    load.start()

    def row_of(xx, yy, cc):
        return (xx * NY + yy) * 2 + cc

    def at(df, ds, cc):
        dx = df * (1 - cc) + ds * cc
        dy = df * cc + ds * (1 - cc)
        return row_of(lax.rem(x + dx + NX, NX), lax.rem(y + dy + NY, NY), cc)

    peers = [
        row_of(lax.rem(x + dx, NX), lax.rem(y + dy, NY), lax.rem(core + dc, 2))
        for dx in (2, 1, 3, 0) for dy in (2, 1, 3, 0) for dc in (0, 1) if dx or dy or dc
    ]
    z_next = lax.rem(z + 1, NZ)
    z_prev = lax.rem(z + NZ - 1, NZ)
    sibling = row_of(x, y, 1 - core)

    barrier = pltpu.get_barrier_semaphore()
    for peer in peers:
        pl.semaphore_signal(barrier, inc=1, device_id=(peer, z), device_id_type=MESH)
    for peer in (z_next, z_prev):
        pl.semaphore_signal(barrier, inc=1, device_id=(row, peer), device_id_type=MESH)
    cells = jnp.where(
        lax.broadcasted_iota(jnp.int32, (1, sim.shape[1]), 1) < TILE, pat_ref[0, 0], pat_ref[0, 1]
    ).astype(jnp.float32)
    load.wait()
    part = jnp.sum(sim[...], axis=0, keepdims=True) * cells
    pl.semaphore_wait(barrier, len(peers) + 2)

    pending = []

    def send(src, dst, send_sem, recv_sem, to):
        copy = pltpu.make_async_remote_copy(
            src_ref=src, dst_ref=dst, send_sem=send_sem, recv_sem=recv_sem,
            device_id=to, device_id_type=MESH,
        )
        copy.start()
        pending.append(copy)
        return copy

    def plane_sum(value, parts, base):
        parts[row] = value
        copies = [
            send(parts.at[row], parts.at[row], p_send.at[base + i], p_recv.at[base + i], (peer, z))
            for i, peer in enumerate(peers)
        ]
        if base:
            for copy in pending[:-len(copies)]:
                copy.wait_send()
            del pending[:-len(copies)]
        for copy in copies:
            copy.wait_recv()
        return jnp.sum(parts[...], axis=0)

    ways = ((1, z_next), (-1, z_prev))
    raw_copies = [
        send(sim.at[pl.ds(w * HALF, HALF)], raw.at[w], r_send.at[w], r_recv.at[w], (row, peer))
        for w, (_, peer) in enumerate(ways)
    ]

    total = plane_sum(part, p1, 0)
    scale = cells * (total_rows / total)
    scales[2] = scale
    scale_copies = [
        send(scales.at[2], scales.at[w], c_send.at[w], c_recv.at[w], (row, peer))
        for w, (_, peer) in enumerate(ways)
    ]
    operand = (sim[...] * scale).astype(jnp.bfloat16)
    left[z] = operand

    def block(r):
        return right.at[r // 2, pl.ds(lax.rem(r, 2) * TILE, TILE)]

    right[chip, pl.ds(core * TILE, TILE)] = operand

    last = NZ - 2
    z_copies = {}

    def z_hop(way, j):
        origin = lax.rem(z - way * (j // 2) + NZ, NZ)
        half = j % 2 if way > 0 else 1 - j % 2
        ref = left.at[origin, pl.ds(half * HALF, HALF)]
        w = 0 if way > 0 else 1
        z_copies[way, j] = send(ref, ref, z_send.at[w, j], z_recv.at[w, j], (row, z_next if way > 0 else z_prev))

    def z_take(way, j):
        if j == 0:
            w = 0 if way > 0 else 1
            raw_copies[w].wait_recv()
            scale_copies[w].wait_recv()
            left[z_prev if way > 0 else z_next, pl.ds(w * HALF, HALF)] = (raw[w] * scales[w]).astype(jnp.bfloat16)
        else:
            z_copies[way, j].wait_recv()
        if j + 2 <= last:
            z_hop(way, j + 2)

    plane = {}

    def plane_hop(df, ds, sems, to_f, to_s, key):
        ref = block(at(df, ds, core))
        plane[key] = send(ref, ref, sems[0], sems[1], (at(to_f, to_s, core), z))

    def f_hop(i, df, way):
        plane_hop(df, 0, (f_send.at[i], f_recv.at[i]), way, 0, ("f", i))

    def s_hop(g, i, ds, way):
        plane_hop(F_OFF[g], ds, (s_send.at[g, i], s_recv.at[g, i]), 0, way, ("s", g, i))

    to_sibling = []

    def share(df, ds):
        i = len(to_sibling)
        ref = block(at(df, ds, core))
        to_sibling.append(send(ref, ref, d_send.at[i], d_recv.at[i], (sibling, z)))

    def spread(g):
        s_hop(g, 0, 0, 1)
        s_hop(g, 1, 0, -1)

    def arrive(key):
        plane[key].wait_recv()
        if key[0] == "f":
            i = key[1]
            if i == 0:
                f_hop(2, -1, 1)
                share(-1, 0)
                spread(1)
            elif i == 1:
                share(1, 0)
                spread(2)
            else:
                share(-2, 0)
                spread(3)
        else:
            _, g, i = key
            way = FORWARD[g]
            if i == 2:
                share(F_OFF[g], -2 * way)
                return
            ds = -1 if i == 0 else 1
            if ds == -way:
                s_hop(g, 2, ds, way)
            share(F_OFF[g], ds)

    z_hop(1, 1)
    z_hop(-1, 1)
    f_hop(0, 0, 1)
    f_hop(1, 0, -1)
    spread(0)
    share(0, 0)

    def products(first, count):
        def body(i, carry):
            k = lax.rem(z + first + NZ + i, NZ)
            acc[...] += jnp.dot(left[k], right[k], preferred_element_type=jnp.float32)
            return carry
        lax.fori_loop(0, count, body, 0)

    acc[...] = jnp.zeros_like(acc)

    after = {
        3: [("f", 0), ("f", 1), ("s", 0, 0), ("s", 0, 1)],
        5: [("s", 1, 1)],
        6: [("f", 2), ("s", 0, 2), ("s", 2, 1)],
        7: [("s", 1, 0), ("s", 1, 2)],
        8: [("s", 3, 1), ("s", 2, 0)],
        9: [("s", 3, 0), ("s", 3, 2)],
        10: [("s", 2, 2)],
    }
    compute = {
        11: [(-2, 5)],
        12: [(3, 3), (-5, 3)],
        13: [(6, 2), (-7, 2)],
    }
    for j in range(last + 1):
        ready = after.get(j, ())
        z_take(-1, j)
        for key in ready[:len(ready) // 2]:
            arrive(key)
        z_take(1, j)
        for key in ready[len(ready) // 2:]:
            arrive(key)
        if j == 11:
            for copy in to_sibling:
                copy.wait_recv()
        for first, count in compute.get(j, ()):
            products(first, count)

    k = lax.rem(z + NZ // 2, NZ)
    column_sum = jnp.zeros((1, sim.shape[1]), jnp.float32)
    for h in range(2):
        rows = pl.ds(h * HALF, HALF)
        final = acc[rows] + jnp.dot(left[k, rows], right[k], preferred_element_type=jnp.float32)
        final = jnp.square(final * cells)
        acc[rows] = final
        column_sum += jnp.sum(final, axis=0, keepdims=True)
    sums = plane_sum(column_sum, p2, len(peers))
    scale_ref[...] = total_rows / sums

    for copy in pending:
        copy.wait_send()


def shards(similarity, pattern):
    rows, columns = similarity.shape
    dma = pltpu.SemaphoreType.DMA
    planes = NX * NY * 2
    inflated, scale = pl.pallas_call(
        kernel,
        out_shape=(
            pltpu.VMEM((rows, columns), jnp.float32),
            pltpu.VMEM((1, columns), jnp.float32),
        ),
        in_specs=[
            pl.BlockSpec(memory_space=pl.ANY),
            pl.BlockSpec(memory_space=pltpu.SMEM),
        ],
        out_specs=(pl.BlockSpec(memory_space=pltpu.VMEM),) * 2,
        scratch_shapes=[
            pltpu.VMEM((rows, columns), jnp.float32),
            pltpu.VMEM((NZ, rows, columns), jnp.bfloat16),
            pltpu.VMEM((NX * NY, 2 * rows, columns), jnp.bfloat16),
            pltpu.VMEM((planes, 1, columns), jnp.float32),
            pltpu.VMEM((planes, 1, columns), jnp.float32),
            pltpu.VMEM((2, HALF, columns), jnp.float32),
            pltpu.VMEM((3, 1, columns), jnp.float32),
            dma, dma((2, NZ - 1)), dma((2, NZ - 1)), dma((2,)), dma((2,)), dma((2,)), dma((2,)),
            dma((3,)), dma((3,)),
            dma((4, 3)), dma((4, 3)), dma((NX * NY,)), dma((NX * NY,)),
            dma((2 * planes - 2,)), dma((2 * planes - 2,)),
        ],
        compiler_params=pltpu.CompilerParams(collective_id=0, has_side_effects=True),
    )(similarity, pattern)
    return inflated * scale


def solution(mesh):
    placed = (P("row", "col"), P("row", "col"))
    return jax.shard_map(
        shards, mesh=mesh, in_specs=placed, out_specs=P("row", "col"), check_vma=False
    )
```

```python
import jax
import jax.numpy as jnp
from jax import lax
from jax.experimental import pallas as pl
from jax.experimental.pallas import tpu as pltpu
from jax.sharding import PartitionSpec as P

MESH = pl.DeviceIdType.MESH
TILE = 256
NX, NY, NZ = 4, 4, 16
HALF = TILE // 2

F_OFF = (0, -1, 1, -2)
FORWARD = (1, -1, 1, -1)


def kernel(
    sim_hbm, pat_ref, acc, scale_ref,
    sim, left, right, p1, p2, raw, scales,
    in_sem, z_send, z_recv, r_send, r_recv, c_send, c_recv, f_send, f_recv, s_send, s_recv, d_send, d_recv,
    p_send, p_recv,
):
    row = lax.axis_index("row")
    z = lax.axis_index("col")
    core = lax.rem(row, 2)
    chip = row // 2
    y = lax.rem(chip, NY)
    x = chip // NY
    total_rows = float(NX * NY * 2 * TILE)

    load = pltpu.make_async_copy(sim_hbm, sim, in_sem)
    load.start()

    def row_of(xx, yy, cc):
        return (xx * NY + yy) * 2 + cc

    def at(df, ds, cc):
        dx = df * (1 - cc) + ds * cc
        dy = df * cc + ds * (1 - cc)
        return row_of(lax.rem(x + dx + NX, NX), lax.rem(y + dy + NY, NY), cc)

    peers = [
        row_of(lax.rem(x + dx, NX), lax.rem(y + dy, NY), lax.rem(core + dc, 2))
        for dx in (2, 1, 3, 0) for dy in (2, 1, 3, 0) for dc in (0, 1) if dx or dy or dc
    ]
    z_next = lax.rem(z + 1, NZ)
    z_prev = lax.rem(z + NZ - 1, NZ)
    sibling = row_of(x, y, 1 - core)

    barrier = pltpu.get_barrier_semaphore()
    for peer in (z_next, z_prev):
        pl.semaphore_signal(barrier, inc=1, device_id=(row, peer), device_id_type=MESH)
    for peer in peers:
        pl.semaphore_signal(barrier, inc=1, device_id=(peer, z), device_id_type=MESH)
    cells = jnp.where(
        lax.broadcasted_iota(jnp.int32, (1, sim.shape[1]), 1) < TILE, pat_ref[0, 0], pat_ref[0, 1]
    ).astype(jnp.float32)
    load.wait()
    part = jnp.sum(sim[...], axis=0, keepdims=True) * cells
    pl.semaphore_wait(barrier, len(peers) + 2)

    pending = []

    def send(src, dst, send_sem, recv_sem, to):
        copy = pltpu.make_async_remote_copy(
            src_ref=src, dst_ref=dst, send_sem=send_sem, recv_sem=recv_sem,
            device_id=to, device_id_type=MESH,
        )
        copy.start()
        pending.append(copy)
        return copy

    def plane_sum(value, parts, base):
        mine = parts.at[pl.ds(row, 1)]
        mine[...] = value
        copies = [
            send(mine, mine, p_send.at[base + i], p_recv.at[base + i], (peer, z))
            for i, peer in enumerate(peers)
        ]
        if base:
            for copy in pending[:-len(copies)]:
                copy.wait_send()
            del pending[:-len(copies)]
        for copy in copies:
            copy.wait_recv()
        return jnp.sum(parts[...], axis=0, keepdims=True)

    ways = ((1, z_next), (-1, z_prev))
    raw_copies = [
        send(sim.at[pl.ds(w * HALF, HALF)], raw.at[w], r_send.at[w], r_recv.at[w], (row, peer))
        for w, (_, peer) in enumerate(ways)
    ]

    total = plane_sum(part, p1, 0)
    scale = cells * (total_rows / total)
    scales[2] = scale
    scale_copies = [
        send(scales.at[2], scales.at[w], c_send.at[w], c_recv.at[w], (row, peer))
        for w, (_, peer) in enumerate(ways)
    ]
    operand = (sim[...] * scale).astype(jnp.bfloat16)
    left[z] = operand

    def block(r):
        return right.at[r // 2, pl.ds(lax.rem(r, 2) * TILE, TILE)]

    right[chip, pl.ds(core * TILE, TILE)] = operand

    last = NZ - 2
    z_copies = {}

    def z_hop(way, j):
        origin = lax.rem(z - way * (j // 2) + NZ, NZ)
        half = j % 2 if way > 0 else 1 - j % 2
        ref = left.at[origin, pl.ds(half * HALF, HALF)]
        w = 0 if way > 0 else 1
        z_copies[way, j] = send(ref, ref, z_send.at[w, j], z_recv.at[w, j], (row, z_next if way > 0 else z_prev))

    def z_take(way, j):
        if j == 0:
            w = 0 if way > 0 else 1
            raw_copies[w].wait_recv()
            scale_copies[w].wait_recv()
            left[z_prev if way > 0 else z_next, pl.ds(w * HALF, HALF)] = (raw[w] * scales[w]).astype(jnp.bfloat16)
        else:
            z_copies[way, j].wait_recv()
        if j + 2 <= last:
            z_hop(way, j + 2)

    plane = {}

    def plane_hop(df, ds, sems, to_f, to_s, key):
        ref = block(at(df, ds, core))
        plane[key] = send(ref, ref, sems[0], sems[1], (at(to_f, to_s, core), z))

    def f_hop(i, df, way):
        plane_hop(df, 0, (f_send.at[i], f_recv.at[i]), way, 0, ("f", i))

    def s_hop(g, i, ds, way):
        plane_hop(F_OFF[g], ds, (s_send.at[g, i], s_recv.at[g, i]), 0, way, ("s", g, i))

    to_sibling = []

    def share(df, ds):
        i = len(to_sibling)
        ref = block(at(df, ds, core))
        to_sibling.append(send(ref, ref, d_send.at[i], d_recv.at[i], (sibling, z)))

    def spread(g):
        s_hop(g, 0, 0, 1)
        s_hop(g, 1, 0, -1)

    def arrive(key):
        plane[key].wait_recv()
        if key[0] == "f":
            i = key[1]
            if i == 0:
                f_hop(2, -1, 1)
                share(-1, 0)
                spread(1)
            elif i == 1:
                share(1, 0)
                spread(2)
            else:
                share(-2, 0)
                spread(3)
        else:
            _, g, i = key
            way = FORWARD[g]
            if i == 2:
                share(F_OFF[g], -2 * way)
                return
            ds = -1 if i == 0 else 1
            if ds == -way:
                s_hop(g, 2, ds, way)
            share(F_OFF[g], ds)

    z_hop(1, 1)
    z_hop(-1, 1)
    f_hop(0, 0, 1)
    f_hop(1, 0, -1)
    spread(0)
    share(0, 0)

    def products(first, count):
        def body(i, carry):
            k = lax.rem(z + first + NZ + i, NZ)
            acc[...] += jnp.dot(left[k], right[k], preferred_element_type=jnp.float32)
            return carry
        lax.fori_loop(0, count, body, 0)

    acc[...] = jnp.zeros_like(acc)

    after = {
        3: [("f", 0), ("f", 1), ("s", 0, 0), ("s", 0, 1)],
        5: [("s", 1, 1)],
        6: [("f", 2), ("s", 0, 2), ("s", 2, 1)],
        7: [("s", 1, 0), ("s", 1, 2)],
        8: [("s", 3, 1), ("s", 2, 0)],
        9: [("s", 3, 0), ("s", 3, 2)],
        10: [("s", 2, 2)],
    }
    compute = {
        11: [(-2, 5)],
        12: [(3, 3), (-5, 3)],
        13: [(6, 2), (-7, 2)],
    }
    for j in range(last + 1):
        ready = after.get(j, ())
        z_take(-1, j)
        for key in ready[:len(ready) // 2]:
            arrive(key)
        z_take(1, j)
        for key in ready[len(ready) // 2:]:
            arrive(key)
        if j == 11:
            for copy in to_sibling:
                copy.wait_recv()
        for first, count in compute.get(j, ()):
            products(first, count)

    k = lax.rem(z + NZ // 2, NZ)
    column_sum = jnp.zeros((1, sim.shape[1]), jnp.float32)
    for h in range(2):
        rows = pl.ds(h * HALF, HALF)
        final = acc[rows] + jnp.dot(left[k, rows], right[k], preferred_element_type=jnp.float32)
        final = jnp.square(final * cells)
        acc[rows] = final
        column_sum += jnp.sum(final, axis=0, keepdims=True)
    sums = plane_sum(column_sum, p2, len(peers))
    scale_ref[...] = total_rows / sums

    for copy in pending:
        copy.wait_send()


def shards(similarity, pattern):
    rows, columns = similarity.shape
    dma = pltpu.SemaphoreType.DMA
    planes = NX * NY * 2
    inflated, scale = pl.pallas_call(
        kernel,
        out_shape=(
            pltpu.VMEM((rows, columns), jnp.float32),
            pltpu.VMEM((1, columns), jnp.float32),
        ),
        in_specs=[
            pl.BlockSpec(memory_space=pl.ANY),
            pl.BlockSpec(memory_space=pltpu.SMEM),
        ],
        out_specs=(pl.BlockSpec(memory_space=pltpu.VMEM),) * 2,
        scratch_shapes=[
            pltpu.VMEM((rows, columns), jnp.float32),
            pltpu.VMEM((NZ, rows, columns), jnp.bfloat16),
            pltpu.VMEM((NX * NY, 2 * rows, columns), jnp.bfloat16),
            pltpu.VMEM((planes, columns), jnp.float32),
            pltpu.VMEM((planes, columns), jnp.float32),
            pltpu.VMEM((2, HALF, columns), jnp.float32),
            pltpu.VMEM((3, 1, columns), jnp.float32),
            dma, dma((2, NZ - 1)), dma((2, NZ - 1)), dma((2,)), dma((2,)), dma((2,)), dma((2,)),
            dma((3,)), dma((3,)),
            dma((4, 3)), dma((4, 3)), dma((NX * NY,)), dma((NX * NY,)),
            dma((2 * planes - 2,)), dma((2 * planes - 2,)),
        ],
        compiler_params=pltpu.CompilerParams(collective_id=0, has_side_effects=True),
    )(similarity, pattern)
    return inflated * scale


def solution(mesh):
    placed = (P("row", "col"), P("row", "col"))
    return jax.shard_map(
        shards, mesh=mesh, in_specs=placed, out_specs=P("row", "col"), check_vma=False
    )
```
